32 devices in a mesh: rep: 2 (over x), ea: 16 (over z, y, core).
Axes of the slice: x: 2, y: 2, z: 4, core: 2. Of those that a mesh axis runs over, the one named last changes fastest.
Arguments:
- hidden_in: bfloat16 [512, 4, 4096], P('ea', 'rep'), parts along dimension 1, may hold values from -3 to 3
- queries: bfloat16 [32, 512, 512], P(('rep', 'ea')), parts along dimension 0, may hold values from -112 to 112, as said below
- cache_keys: bfloat16 [32, 512, 128], P(('rep', 'ea')), parts along dimension 0, may hold values from -4 to 4
- cache_values: bfloat16 [32, 512, 128], P(('rep', 'ea')), parts along dimension 0, may hold values from -24 to 24
- new_keys: bfloat16 [32, 512, 128], P(('rep', 'ea')), parts along dimension 0, may hold values from -6 to 6
- new_values: bfloat16 [32, 512, 128], P(('rep', 'ea')), parts along dimension 0, may hold values from -24 to 24
- cache_len: int32 [4], P('rep'), parts along dimension 0, may hold values from 128 to 512, as said below
- out_proj: bfloat16 [4096, 4096], P(None, 'ea'), may hold values from -0.25 to 0.25
- norm_gain: float32 [4096], replicated, may hold values from 0.25 to 1.75
- router: bfloat16 [4096, 16], replicated, may hold values from -0.09375 to 0.09375
- expert_ids: int32 [512, 4, 2], P('ea', 'rep'), parts along dimension 1, may hold values from 0 to 15, all different within a row; in each aligned block of 64 rows (0 to 63, 64 to 127, ..., all dimensions but the last counted through in order) at most 9 rows name the same one
- gate_proj: bfloat16 [4096, 51200], P(None, 'ea'), may hold values from -0.09375 to 0.09375
- up_proj: bfloat16 [4096, 51200], P(None, 'ea'), may hold values from -0.09375 to 0.09375
- down_proj: bfloat16 [51200, 4096], P('ea'), may hold values from -0.109375 to 0.109375
Outputs:
- layer_out: bfloat16 [512, 4, 4096], P('ea', 'rep'), parts along dimension 1
The draws below stay inside these ranges and needn't reach their ends.
There are 2 independent parts, one for each index of `rep`. The reference program is written for one: setup_inputs(seed, part) draws one part's arguments, and reference() takes and returns one part's arrays. A program takes and returns all parts, laid end to end along the dimension named above; an argument that names none is the same for every part. Nothing has to cross between parts.
Inputs may be any that keep to these rules, and one draw needn't show every extreme that they name: `queries`: each entry of the hidden draw may reach the stated range. `cache_len`: some sequence has exactly 512 filled slots. `expert_ids`: the two experts of a row differ. Rows are taken in order of the first two dimensions; in each aligned block of 64 rows (the rows of one device) no expert is named by more than 9 rows, and in some block one expert is named by exactly 9 rows; every expert is named somewhere.
All inputs are finite; a program needn't handle non-finite values.
Results may differ from the reference program's by a relative error of at most 0.0068.
Values may be sent and summed in bfloat16 or wider, within the bound.
A program may use at most 192 MiB of HBM per device.

```python
import math
import jax
import jax.numpy as jnp
import numpy as np
from jax import lax

D = 4096
HQ = 32
KVH = 8
HD = 128
EXPERTS = 16
FFW = 3200
TOPK = 2
CACHE = 512
NEW = 512
SEQS = 2
TOK_DEV = 64
CAP = 9
N_EA = 16


def cache_key_base(key):
    base = jax.random.normal(jax.random.fold_in(key, 7), (SEQS * KVH, CACHE, HD), jnp.float32)
    return jnp.clip(base, -4.0, 4.0)


def draw_cache_keys(key, part):
    base = cache_key_base(key)
    return base.astype(jnp.bfloat16)


def draw_queries(key, part):
    base = jax.random.normal(jax.random.fold_in(key, 11), (SEQS * KVH, NEW, HQ // KVH * HD), jnp.float32)
    base = jnp.clip(base, -4.5, 4.5)
    return base.astype(jnp.bfloat16)


def draw_cache_len(key, part):
    filled = jax.random.randint(jax.random.fold_in(key, 3), (SEQS,), CACHE // 4, CACHE + 1)
    longest = jax.random.randint(jax.random.fold_in(key, 5), (), 0, SEQS)
    return filled.at[longest].set(CACHE).astype(jnp.int32)


def shard_levels(stream_key, dims, split, smallest, largest):
    gain, own = 1.0, jax.random.fold_in(stream_key, 6)
    for axis_at, shards_of in split:
        heights = jnp.exp(jax.random.uniform(jax.random.fold_in(own, axis_at), (shards_of,), jnp.float32, smallest / len(split), largest / len(split)))
        gain = gain * jnp.repeat(heights, dims[axis_at] // shards_of).reshape([-1 if axis == axis_at else 1 for axis in range(len(dims))])
    return gain


def deal_out(rng, own, number, rows, amount, top, most, slope):
    order = jax.random.permutation(rng, amount)
    packed, ordinary = portions_of(amount, rows * top, most, slope, True), portions_of(amount, rows * top, most, slope, False)
    places = jnp.arange(amount)

    def named(tallies, turn):
        used = int((tallies > 0).sum())
        fixed = max(1, used // 4)
        moved = fixed + (places - fixed + turn * (used - fixed)) % max(1, amount - fixed)
        return jnp.zeros((amount,), jnp.int32).at[order[jnp.where(places < fixed, places, moved)]].set(jnp.asarray(tallies, jnp.int32))

    tallies = jnp.where(number % 4 == 0, named(packed, number // 4), named(ordinary, number - number // 4 - 1))
    mixed = jax.random.permutation(jax.random.fold_in(own, 3), amount)
    giver, sink = mixed[0:amount // 2 * 2:2], mixed[1:amount // 2 * 2:2]
    margin = jnp.minimum(tallies[giver] - 1, most - tallies[sink]) // 2
    margin = jnp.where((giver == order[0]) | (sink == order[0]) | (tallies[sink] == 0), 0, jnp.maximum(margin, 0))
    moved = jax.random.randint(jax.random.fold_in(own, 4), (amount // 2,), 0, 1 << 20) % (margin + 1)
    tallies = tallies.at[giver].add(-moved).at[sink].add(moved)
    labels = jnp.searchsorted(jnp.cumsum(tallies), jnp.arange(rows * top), side="right").astype(jnp.int32)
    listing = labels.reshape(top, rows).T
    listing = listing[jax.random.permutation(jax.random.fold_in(own, 1), rows)]
    turn = jax.random.randint(jax.random.fold_in(own, 2), (rows, 1), 0, top)
    return jnp.take_along_axis(listing, (jnp.arange(top)[None, :] + turn) % top, axis=1)


def portions_of(amount, total, limit, lean, full):
    weights = [(1 << 20) // math.isqrt(standing ** lean) + 1 for standing in range(1, amount + 1)]
    largest = limit if full else min(limit, max(-(-total // amount), total * weights[0] // sum(weights)))
    least = 1 if total - largest >= amount - 1 else 0
    holding, rest = [largest] + [least] * (amount - 1), total - largest - least * (amount - 1)
    while rest > 0:
        candidates = [i for i in range(1, amount) if holding[i] < largest] or [i for i in range(1, amount) if holding[i] < limit]
        mass, remaining = sum([weights[i] for i in candidates]), rest
        for i in candidates:
            extra = min(limit - holding[i], max(1, remaining * weights[i] // mass), rest)
            holding[i] = holding[i] + extra
            rest = rest - extra
    return np.array(holding)


def centred(rng, dims, scale, bound, split=(), kind=jnp.bfloat16):
    entries = jax.random.normal(rng, dims, jnp.float32) * scale
    if len(split) > 0:
        entries = shard_levels(rng, dims, split, -0.22, 0.18) * entries
    return jnp.clip(entries, min=-bound, max=bound).astype(kind)


def setup_inputs(seed: int = 0, part: int = 0) -> dict:
    keys = jax.random.split(jax.random.key(seed), 15)
    part_keys = jax.random.split(jax.random.fold_in(keys[14], part), 15)
    hidden_in = centred(part_keys[0], (NEW, SEQS, D), 0.5, 3.0, ((0, 16),))
    queries = draw_queries(jax.random.fold_in(jax.random.fold_in(keys[14], part), 71), part)
    cache_keys = draw_cache_keys(jax.random.fold_in(jax.random.fold_in(keys[14], part), 71), part)
    cache_values = centred(part_keys[3], (SEQS * KVH, CACHE, HD), 4.0, 24.0, ((0, 16),))
    new_keys = centred(part_keys[4], (SEQS * KVH, NEW, HD), 1.0, 6.0, ((0, 16),))
    new_values = centred(part_keys[5], (SEQS * KVH, NEW, HD), 4.0, 24.0, ((0, 16),))
    cache_len = draw_cache_len(jax.random.fold_in(jax.random.fold_in(keys[14], part), 71), part)
    out_proj = centred(keys[7], (HQ * HD, D), (HQ * HD // 8) ** -0.5, 0.25, ((1, 16),))
    norm_gain = jnp.clip(1.0 + 0.15 * jax.random.normal(keys[8], (D,), jnp.float32), 0.25, 1.75)
    router = centred(keys[9], (D, EXPERTS), D ** -0.5, 0.09375)
    expert_ids_keys = jax.random.split(jax.random.fold_in(part_keys[10], 1), NEW * SEQS // TOK_DEV)
    expert_ids_turns = jax.random.permutation(jax.random.fold_in(part_keys[10], 3), NEW * SEQS // TOK_DEV)
    expert_ids = jax.vmap(lambda own, number: deal_out(jax.random.fold_in(part_keys[10], 2), own, number, TOK_DEV, EXPERTS, TOPK, CAP, 2))(expert_ids_keys, expert_ids_turns).reshape((NEW, SEQS, TOPK))
    gate_proj = centred(keys[11], (D, EXPERTS * FFW), D ** -0.5, 0.09375, ((1, 16),))
    up_proj = centred(keys[12], (D, EXPERTS * FFW), D ** -0.5, 0.09375, ((1, 16),))
    down_proj = centred(keys[13], (EXPERTS * FFW, D), FFW ** -0.5, 0.109375, ((0, 16),))
    return {"hidden_in": hidden_in, "queries": queries, "cache_keys": cache_keys, "cache_values": cache_values, "new_keys": new_keys, "new_values": new_values, "cache_len": cache_len, "out_proj": out_proj, "norm_gain": norm_gain, "router": router, "expert_ids": expert_ids, "gate_proj": gate_proj, "up_proj": up_proj, "down_proj": down_proj}


def reference(hidden_in, queries, cache_keys, cache_values, new_keys, new_values, cache_len, out_proj, norm_gain, router, expert_ids, gate_proj, up_proj, down_proj):
    group_q = HQ // KVH
    seq_count = N_EA // KVH
    shard_count = N_EA // EXPERTS
    hid_width = FFW // shard_count
    score_scale = 1.0 / math.sqrt(HD)
    position = jnp.arange(NEW, dtype=jnp.int32)
    key_pos = jnp.arange(CACHE + NEW, dtype=jnp.int32)

    def attend(attn_unit):
        query_rows = queries[attn_unit].reshape(NEW, group_q, HD).astype(jnp.float32)
        all_keys = jnp.concatenate([cache_keys[attn_unit], new_keys[attn_unit]], axis=0).astype(jnp.float32)
        all_values = jnp.concatenate([cache_values[attn_unit], new_values[attn_unit]], axis=0).astype(jnp.float32)
        visible = cache_len[attn_unit // KVH]
        allowed = jnp.where(key_pos[None, :] < CACHE, key_pos[None, :] < visible, key_pos[None, :] - CACHE <= position[:, None])
        scores = jnp.einsum('qhd,kd->hqk', query_rows, all_keys) * score_scale
        scores = jnp.where(allowed[None], scores, jnp.float32(-1e+30))
        top_score = lax.optimization_barrier(jnp.max(scores, axis=2, keepdims=True))
        exp_scores = jnp.exp(scores - top_score)
        attn_probs = lax.optimization_barrier((exp_scores / lax.optimization_barrier(jnp.sum(exp_scores, axis=2, keepdims=True))).astype(jnp.bfloat16))
        attended = jnp.einsum('hqk,kd->qhd', attn_probs.astype(jnp.float32), all_values).astype(jnp.bfloat16).reshape(NEW, group_q * HD)
        group_proj = lax.dynamic_slice_in_dim(out_proj, attn_unit % KVH * group_q * HD, group_q * HD, 0)
        return jnp.dot(attended, group_proj, preferred_element_type=jnp.float32).astype(jnp.bfloat16)
    head_terms = lax.optimization_barrier(lax.map(attend, jnp.arange(N_EA, dtype=jnp.int32)))
    head_sum = lax.optimization_barrier(jnp.sum(head_terms.reshape(seq_count, KVH, NEW, D).astype(jnp.float32), axis=1))
    residual = hidden_in.astype(jnp.float32) + jnp.transpose(head_sum, (1, 0, 2))
    flat_res = residual.reshape(NEW * seq_count, D)
    mean_sq = lax.optimization_barrier(jnp.mean(flat_res * flat_res, axis=1, keepdims=True))
    normed = (flat_res * lax.rsqrt(mean_sq + 1e-05) * norm_gain[None, :]).astype(jnp.bfloat16)
    logits = jnp.dot(normed, router, preferred_element_type=jnp.float32)
    route_ids = expert_ids.reshape(NEW * seq_count, TOPK)
    chosen = jnp.take_along_axis(logits, route_ids, axis=1)
    first_gate = jax.nn.sigmoid(chosen[:, 0:1] - chosen[:, 1:2])
    flat_ids = route_ids.reshape(-1)
    capacity = N_EA * CAP
    one_hot = (flat_ids[:, None] == jnp.arange(EXPERTS, dtype=jnp.int32)[None, :]).astype(jnp.int32)
    slot_rank = lax.optimization_barrier(jnp.sum((jnp.cumsum(one_hot, axis=0) - one_hot) * one_hot, axis=1)).astype(jnp.int32)

    def run_expert(expert):
        members = jnp.argsort((flat_ids != expert).astype(jnp.int32), stable=True)[:capacity]
        routed_rows = normed[members // TOPK]
        gate_cols = lax.dynamic_slice_in_dim(gate_proj, expert * FFW, FFW, 1)
        up_cols = lax.dynamic_slice_in_dim(up_proj, expert * FFW, FFW, 1)
        gate_val = jnp.dot(routed_rows, gate_cols, preferred_element_type=jnp.float32)
        up_val = jnp.dot(routed_rows, up_cols, preferred_element_type=jnp.float32)
        inner_act = (jax.nn.silu(gate_val) * up_val).astype(jnp.bfloat16)
        shard_total = jnp.zeros((capacity, D), jnp.float32)
        for shard_num in range(shard_count):
            down_rows = lax.dynamic_slice_in_dim(down_proj, expert * FFW + shard_num * hid_width, hid_width, 0)
            shard_term = jnp.dot(inner_act[:, shard_num * hid_width:(shard_num + 1) * hid_width], down_rows, preferred_element_type=jnp.float32).astype(jnp.bfloat16)
            shard_total = shard_total + lax.optimization_barrier(shard_term).astype(jnp.float32)
        return shard_total
    expert_out = lax.map(run_expert, jnp.arange(EXPERTS, dtype=jnp.int32))
    picked = expert_out[flat_ids, slot_rank].reshape(NEW * seq_count, TOPK, D)
    mixed = flat_res + first_gate * picked[:, 0] + (1.0 - first_gate) * picked[:, 1]
    return mixed.astype(jnp.bfloat16).reshape(NEW, seq_count, D)
```

```python
import functools
import math

import jax
import jax.numpy as jnp
from jax import lax
from jax.experimental import pallas as pl
from jax.experimental.pallas import tpu as pltpu
from jax.sharding import PartitionSpec as P

HQ = 32
KVH = 8
HD = 128
EXPERTS = 16
TOPK = 2
CAP = 9


def expert_terms(received, gate_proj, up_proj, down_proj):
    src_count, slot_count, model_width = received.shape
    flat_rows = received.reshape(src_count * slot_count, model_width)
    gate_val = jnp.dot(flat_rows, gate_proj, preferred_element_type=jnp.float32)
    up_val = jnp.dot(flat_rows, up_proj, preferred_element_type=jnp.float32)
    inner_act = (jax.nn.silu(gate_val) * up_val).astype(jnp.bfloat16)
    shard_term = jnp.dot(inner_act, down_proj, preferred_element_type=jnp.float32).astype(
        jnp.bfloat16
    )
    return shard_term.reshape(src_count, slot_count, model_width)


def expert_half(received, gate_proj, up_proj, down_proj):
    shard_term = expert_terms(received, gate_proj, up_proj, down_proj)
    return lax.all_to_all(shard_term, "ea", split_axis=0, concat_axis=0, tiled=True)


def route_rows(normed, route_ids, first_gate, gate_proj, up_proj, down_proj):
    row_count, model_width = normed.shape
    dev_count = lax.axis_size("ea")
    shard_count = dev_count // EXPERTS
    flat_ids = route_ids.reshape(-1)
    pair_count = flat_ids.shape[0]
    expert_cols = jnp.arange(EXPERTS, dtype=jnp.int32)
    one_hot = (flat_ids[:, None] == expert_cols[None, :]).astype(jnp.float32)
    pair_order = jnp.arange(pair_count, dtype=jnp.int32)
    earlier = (pair_order[:, None] > pair_order[None, :]).astype(jnp.float32)
    before = jnp.dot(earlier, one_hot, precision=lax.Precision.HIGHEST)
    slot_pos = jnp.sum(before * one_hot, axis=1).astype(jnp.int32)
    target = (flat_ids * CAP + slot_pos).reshape(row_count, TOPK)
    slot_ids = jnp.arange(EXPERTS * CAP, dtype=jnp.int32)
    select = (
        (target[None, :, 0] == slot_ids[:, None]) | (target[None, :, 1] == slot_ids[:, None])
    ).astype(jnp.bfloat16)
    packed = jnp.dot(select, normed, preferred_element_type=jnp.float32).astype(jnp.bfloat16)
    packed = jnp.broadcast_to(
        packed.reshape(EXPERTS, 1, CAP, model_width), (EXPERTS, shard_count, CAP, model_width)
    )
    packed = packed.reshape(dev_count, CAP, model_width)
    first_slots = (CAP + 1) // 2
    bounds = [(0, first_slots), (first_slots, CAP)]
    pieces = []
    for lower, upper in bounds:
        part_block = packed[:, lower:upper]
        pieces.append(
            (lambda received: expert_half(received, gate_proj, up_proj, down_proj))(
                lax.all_to_all(part_block, "ea", split_axis=0, concat_axis=0, tiled=True)
            )
        )
    returned = jnp.concatenate(pieces, axis=1)
    expert_out = jnp.sum(
        returned.reshape(EXPERTS, shard_count, CAP, model_width).astype(jnp.float32), axis=1
    )
    expert_out = expert_out.reshape(EXPERTS * CAP, model_width)
    picked = jnp.take(expert_out, target, axis=0)
    return first_gate * picked[:, 0] + (1.0 - first_gate) * picked[:, 1]


def wide_body(
    hidden_in,
    queries,
    cache_keys,
    cache_values,
    new_keys,
    new_values,
    cache_len,
    out_proj,
    norm_gain,
    router,
    expert_ids,
    gate_proj,
    up_proj,
    down_proj,
):
    dev_count = lax.axis_size("ea")
    dev_index = lax.axis_index("ea")
    new_rows = queries.shape[1]
    group_q = HQ // KVH
    seq_count = dev_count // KVH
    piece_rows = new_rows // dev_count
    cache_rows = cache_keys.shape[1]
    col_width = out_proj.shape[1]
    model_width = hidden_in.shape[2]
    score_scale = 1.0 / math.sqrt(HD)
    visible = lax.dynamic_index_in_dim(cache_len, dev_index // KVH, keepdims=False)
    position = (
        jnp.arange(new_rows, dtype=jnp.int32).reshape(dev_count, piece_rows).T.reshape(new_rows)
    )
    query_rows = (
        queries[0]
        .reshape(dev_count, piece_rows, group_q, HD)
        .transpose(1, 0, 2, 3)
        .reshape(new_rows, group_q, HD)
    )
    all_keys = jnp.concatenate([cache_keys[0], new_keys[0]], axis=0)
    all_values = jnp.concatenate([cache_values[0], new_values[0]], axis=0)
    key_pos = jnp.arange(cache_rows + new_rows, dtype=jnp.int32)
    allowed = jnp.where(
        key_pos[None, :] < cache_rows,
        key_pos[None, :] < visible,
        key_pos[None, :] - cache_rows <= position[:, None],
    )
    scores = (
        jnp.einsum("qhd,kd->hqk", query_rows, all_keys, preferred_element_type=jnp.float32)
        * score_scale
    )
    scores = jnp.where(allowed[None], scores, jnp.float32(-1e30))
    top_score = jnp.max(scores, axis=2, keepdims=True)
    exp_scores = jnp.exp(scores - top_score)
    attn_probs = (exp_scores / jnp.sum(exp_scores, axis=2, keepdims=True)).astype(jnp.bfloat16)
    attended = jnp.einsum("hqk,kd->qhd", attn_probs, all_values, preferred_element_type=jnp.float32)
    attended = attended.astype(jnp.bfloat16).reshape(new_rows, group_q * HD)
    local_rows = out_proj.reshape(KVH, group_q * HD, col_width).transpose(1, 0, 2)
    outgoing = jnp.broadcast_to(local_rows[:, None], (group_q * HD, seq_count, KVH, col_width))
    outgoing = outgoing.reshape(group_q * HD, dev_count, col_width)
    group_proj = lax.all_to_all(outgoing, "ea", split_axis=1, concat_axis=1, tiled=True).reshape(
        group_q * HD, model_width
    )
    head_part = jnp.dot(attended, group_proj, preferred_element_type=jnp.float32).astype(
        jnp.bfloat16
    )
    arrived = lax.all_to_all(
        head_part.reshape(piece_rows, dev_count, model_width),
        "ea",
        split_axis=1,
        concat_axis=1,
        tiled=True,
    )
    head_sum = jnp.sum(
        arrived.reshape(piece_rows, seq_count, KVH, model_width).astype(jnp.float32), axis=2
    )
    residual = hidden_in.astype(jnp.float32) + head_sum
    flat_res = residual.reshape(piece_rows * seq_count, model_width)
    mean_sq = jnp.mean(flat_res * flat_res, axis=1, keepdims=True)
    normed = (flat_res * lax.rsqrt(mean_sq + 1e-05) * norm_gain[None, :]).astype(jnp.bfloat16)
    logits = jnp.dot(normed, router, preferred_element_type=jnp.float32)
    route_ids = expert_ids.reshape(piece_rows * seq_count, TOPK)
    chosen = jnp.take_along_axis(logits, route_ids, axis=1)
    first_gate = jax.nn.sigmoid(chosen[:, 0:1] - chosen[:, 1:2])
    expert_mix = route_rows(normed, route_ids, first_gate, gate_proj, up_proj, down_proj)
    result_rows = (flat_res + expert_mix).astype(jnp.bfloat16)
    return result_rows.reshape(piece_rows, seq_count, model_width)


NZ = 4
NDEV = 16
MAIN = 8
SLOTS = EXPERTS * CAP
F32 = jnp.float32
BF16 = jnp.bfloat16


def attend_kernel(len_ref, q_ref, ck_ref, cv_ref, nk_ref, nv_ref, o_ref, *, seq_devs):
    visible = len_ref[lax.axis_index("ea") // seq_devs]
    contract = (((1,), (1,)), ((), ()))
    q = q_ref[...]
    rows, cached, fresh = q.shape[0], ck_ref.shape[0], nk_ref.shape[0]
    scale = 1.0 / math.sqrt(HD)
    old = lax.dot_general(q, ck_ref[...], contract, preferred_element_type=F32) * scale
    new = lax.dot_general(q, nk_ref[...], contract, preferred_element_type=F32) * scale
    old_pos = lax.broadcasted_iota(jnp.int32, (rows, cached), 1)
    row_pos = lax.broadcasted_iota(jnp.int32, (rows, fresh), 0)
    new_pos = lax.broadcasted_iota(jnp.int32, (rows, fresh), 1)
    old = jnp.where(old_pos < visible, old, -1e30)
    new = jnp.where(new_pos <= row_pos, new, -1e30)
    top = jnp.maximum(
        jnp.max(old, axis=1, keepdims=True), jnp.max(new, axis=1, keepdims=True)
    )
    old = jnp.exp(old - top)
    new = jnp.exp(new - top)
    total = jnp.sum(old, axis=1, keepdims=True) + jnp.sum(new, axis=1, keepdims=True)
    mixed = jnp.dot(old.astype(BF16), cv_ref[...], preferred_element_type=F32)
    mixed += jnp.dot(new.astype(BF16), nv_ref[...], preferred_element_type=F32)
    o_ref[...] = (mixed / total).astype(BF16)


def attend(cache_len, q, ck, cv, nk, nv):
    rows, width = q.shape
    return pl.pallas_call(
        functools.partial(attend_kernel, seq_devs=KVH),
        grid=(width // HD,),
        out_shape=jax.ShapeDtypeStruct((rows, width), BF16),
        in_specs=[
            pl.BlockSpec(memory_space=pltpu.SMEM),
            pl.BlockSpec((rows, HD), lambda h: (0, h)),
            pl.BlockSpec(ck.shape, lambda h: (0, 0)),
            pl.BlockSpec(cv.shape, lambda h: (0, 0)),
            pl.BlockSpec(nk.shape, lambda h: (0, 0)),
            pl.BlockSpec(nv.shape, lambda h: (0, 0)),
        ],
        out_specs=pl.BlockSpec((rows, HD), lambda h: (0, h)),
        compiler_params=pltpu.CompilerParams(vmem_limit_bytes=40 << 20),
    )(cache_len, q, ck, cv, nk, nv)


def remote(src, dst, send, recv, dev):
    return pltpu.make_async_remote_copy(
        src_ref=src,
        dst_ref=dst,
        send_sem=send,
        recv_sem=recv,
        device_id={"ea": dev},
        device_id_type=pl.DeviceIdType.MESH,
    )


def greet(me):
    barrier = pltpu.get_barrier_semaphore()

    def hello(off, carry):
        pl.semaphore_signal(
            barrier,
            inc=1,
            device_id={"ea": lax.rem(me + off, NDEV)},
            device_id_type=pl.DeviceIdType.MESH,
        )
        return carry

    lax.fori_loop(1, NDEV, hello, 0)
    pl.semaphore_wait(barrier, NDEV - 1)


def others(me, step):
    def go(off, carry):
        step(lax.rem(me + off, NDEV))
        return carry

    lax.fori_loop(1, NDEV, go, 0)


def front_kernel(
    att_ref, proj_ref, hid_ref, gain_ref, router_ref, ids_ref,
    res_ref, gate_ref, place_ref, main_ref, extra_ref,
    buf, acc, hs, arrived, normed, send_main, send_extra,
    block_sem, left_sem, right_sem, y_sem, core_sem,
    hs_send, hs_recv, main_send, main_recv, extra_send, extra_recv,
):
    me = lax.axis_index("ea")
    z, y, c = me // 4, (me // 2) % 2, me % 2

    def index(zz, yy, cc):
        return (zz * 2 + yy) * 2 + cc

    buf[me] = att_ref[...]
    acc[...] = jnp.zeros_like(acc)
    greet(me)

    def block_copy(blk, sem, dev):
        return remote(buf.at[blk], buf.at[blk], sem, block_sem.at[blk], dev)

    def to_left(zz):
        return block_copy(index(zz, y, c), left_sem.at[zz], index(z - 1, y, c))

    def to_right(zz):
        return block_copy(index(zz, y, c), right_sem.at[zz], index(z + 1, y, c))

    def to_y(zz):
        return block_copy(index(zz, y, c), y_sem.at[zz], index(z, 1 - y, c))

    def to_core(zz, yy):
        return block_copy(index(zz, yy, c), core_sem.at[zz * 2 + yy], index(z, y, 1 - c))

    def landed(blk):
        remote(buf.at[blk], buf.at[blk], left_sem.at[0], block_sem.at[blk], index(z, y, 1 - c)).wait_recv()

    def line(zz, go_left, go_right):
        if go_left:
            @pl.when(z > 0)
            def _():
                to_left(zz).start()
        if go_right:
            @pl.when(z < NZ - 1)
            def _():
                to_right(zz).start()
        to_y(zz).start()
        to_core(zz, y).start()

    def pair(d, step):
        @pl.when(z + d < NZ)
        def _():
            step(z + d, True)

        @pl.when(z - d >= 0)
        def _():
            step(z - d, False)

    def arrive_line(d):
        def step(zz, from_right):
            landed(index(zz, y, c))
            line(zz, from_right, not from_right)

        pair(d, step)

    def across(zz):
        landed(index(zz, 1 - y, c))
        to_core(zz, 1 - y).start()

    def arrive_y(d):
        if d == 0:
            across(z)
        else:
            pair(d, lambda zz, _: across(zz))

    def multiply(d):
        def go(n, carry):
            side, yy, cc = n % 2, (n // 2) % 2, n // 4
            zz = z + d * (1 - 2 * side)
            ok = (zz >= 0) & (zz < NZ)
            if d == 0:
                ok = ok & (side == 0)

            @pl.when(ok)
            def _():
                blk = index(zz, (y + yy) % 2, (c + cc) % 2)

                @pl.when(cc == 1)
                def _():
                    landed(blk)

                group = blk % KVH
                width = buf.shape[2]
                rows = pl.ds(pl.multiple_of(group * width, width), width)
                acc[blk // KVH] += jnp.dot(
                    buf[blk], proj_ref[rows, :], preferred_element_type=F32
                )

            return carry

        lax.fori_loop(0, 8, go, 0)

    line(z, True, True)

    ids = ids_ref[...]
    lanes = lax.broadcasted_iota(jnp.int32, (ids.shape[0], EXPERTS), 1)
    count = ids.shape[0]
    first = (ids[:, 0:1] == lanes).astype(F32)
    second = (ids[:, 1:2] == lanes).astype(F32)
    tri = (
        lax.broadcasted_iota(jnp.int32, (count, count), 1)
        < lax.broadcasted_iota(jnp.int32, (count, count), 0)
    ).astype(F32)
    before0 = jnp.dot(tri, first, preferred_element_type=F32)
    before1 = jnp.dot(tri, second, preferred_element_type=F32) + jnp.sum(
        first, axis=0, keepdims=True
    )
    slot_lanes = lax.broadcasted_iota(jnp.int32, (count, SLOTS), 1).astype(F32)

    def placing(before, one_hot, col):
        slot = jnp.sum(before * one_hot, axis=1, keepdims=True)
        expert = ids[:, col : col + 1].astype(F32)
        where = jnp.where(slot < MAIN - 0.5, expert * MAIN + slot, EXPERTS * MAIN + expert)
        return (slot_lanes == where).astype(F32)

    place0 = placing(before0, first, 0)
    place1 = placing(before1, second, 1)
    place_ref[0] = place0.astype(BF16)
    place_ref[1] = place1.astype(BF16)

    for d in range(1, NZ):
        arrive_line(d)
        arrive_y(d - 1)
        multiply(d - 1)
    arrive_y(NZ - 1)
    multiply(NZ - 1)

    hs[...] = acc[...].astype(BF16)
    piece = arrived.shape[1]
    width = hs.shape[2]
    col_me = pl.ds(pl.multiple_of(me * width, width), width)
    row_me = pl.ds(pl.multiple_of(me * piece, piece), piece)

    def hs_copy(dev):
        rows = pl.ds(pl.multiple_of(dev * piece, piece), piece)
        return remote(
            hs.at[:, rows, :], arrived.at[:, :, col_me], hs_send.at[dev], hs_recv.at[me], dev
        )

    def hs_landed(dev):
        cols = pl.ds(pl.multiple_of(dev * width, width), width)
        remote(
            hs.at[:, row_me, :], arrived.at[:, :, cols], hs_send.at[dev], hs_recv.at[dev], dev
        ).wait_recv()

    others(me, lambda dev: hs_copy(dev).start())
    arrived[:, :, col_me] = hs[:, row_me, :]
    others(me, hs_landed)

    total = arrived[...].astype(F32).reshape(res_ref.shape)
    residual = hid_ref[...].astype(F32) + total
    res_ref[...] = residual
    mean_sq = jnp.mean(residual * residual, axis=1, keepdims=True)
    normed[...] = (residual * lax.rsqrt(mean_sq + 1e-05) * gain_ref[...]).astype(BF16)
    select = (place0 + place1).T.astype(BF16)
    packed = jnp.dot(select, normed[...], preferred_element_type=F32)
    model = packed.shape[1]
    send_main[...] = packed[: EXPERTS * MAIN].astype(BF16).reshape(NDEV, MAIN, model)
    send_extra[...] = packed[EXPERTS * MAIN :].reshape(NDEV, 1, model)

    def main_copy(src, dst, dev):
        return remote(send_main.at[dev], main_ref.at[src], main_send.at[dev], main_recv.at[src], dev)

    def extra_copy(src, dst, dev):
        return remote(
            send_extra.at[dev], extra_ref.at[src], extra_send.at[dev], extra_recv.at[src], dev
        )

    def dispatch(dev):
        main_copy(me, dev, dev).start()
        extra_copy(me, dev, dev).start()

    others(me, dispatch)
    main_ref[me] = send_main[me]
    extra_ref[me] = send_extra[me]
    logits = jnp.dot(normed[...], router_ref[...], preferred_element_type=F32)
    gap = jnp.sum(logits * first, axis=1, keepdims=True) - jnp.sum(
        logits * second, axis=1, keepdims=True
    )
    gate_ref[...] = jnp.broadcast_to(jax.nn.sigmoid(gap), gate_ref.shape)

    def finish(dev):
        main_copy(dev, me, dev).wait_recv()
        extra_copy(dev, me, dev).wait_recv()
        main_copy(me, dev, dev).wait_send()
        extra_copy(me, dev, dev).wait_send()
        hs_copy(dev).wait_send()

    others(me, finish)
    for zz in range(NZ):
        @pl.when((z > 0) & (zz >= z))
        def _():
            to_left(zz).wait_send()

        @pl.when((z < NZ - 1) & (zz <= z))
        def _():
            to_right(zz).wait_send()

        to_y(zz).wait_send()
        to_core(zz, 0).wait_send()
        to_core(zz, 1).wait_send()


def vmem(count):
    return [pl.BlockSpec(memory_space=pltpu.VMEM)] * count


def front(attended, out_proj, hidden, gain, router, ids):
    rows, width = attended.shape
    seqs = NDEV // KVH
    cols = out_proj.shape[1]
    mine, model = hidden.shape
    dma = pltpu.SemaphoreType.DMA
    return pl.pallas_call(
        front_kernel,
        out_shape=[
            jax.ShapeDtypeStruct((mine, model), F32),
            jax.ShapeDtypeStruct((mine, 128), F32),
            jax.ShapeDtypeStruct((2, mine, SLOTS), BF16),
            jax.ShapeDtypeStruct((NDEV, MAIN, model), BF16),
            jax.ShapeDtypeStruct((NDEV, 1, model), F32),
        ],
        in_specs=vmem(6),
        out_specs=vmem(5),
        scratch_shapes=[
            pltpu.VMEM((NDEV, rows, width), BF16),
            pltpu.VMEM((seqs, rows, cols), F32),
            pltpu.VMEM((seqs, rows, cols), BF16),
            pltpu.VMEM((seqs, rows // NDEV, model), BF16),
            pltpu.VMEM((mine, model), BF16),
            pltpu.VMEM((NDEV, MAIN, model), BF16),
            pltpu.VMEM((NDEV, 1, model), F32),
            dma((NDEV,)), dma((NZ,)), dma((NZ,)), dma((NZ,)), dma((2 * NZ,)),
            dma((NDEV,)), dma((NDEV,)), dma((NDEV,)), dma((NDEV,)), dma((NDEV,)), dma((NDEV,)),
        ],
        compiler_params=pltpu.CompilerParams(
            collective_id=0, has_side_effects=True, vmem_limit_bytes=50 << 20
        ),
    )(attended, out_proj, hidden, gain, router, ids)


def expert_kernel(main_ref, extra_ref, gate_ref, up_ref, down_ref, omain_ref, oextra_ref, x, acc):
    step = pl.program_id(0)
    cut = EXPERTS * MAIN

    @pl.when(step == 0)
    def _():
        x[:cut] = main_ref[...].reshape(cut, x.shape[1])
        x[cut:] = extra_ref[...].reshape(EXPERTS, x.shape[1]).astype(BF16)
        acc[...] = jnp.zeros_like(acc)

    gate = jnp.dot(x[...], gate_ref[...], preferred_element_type=F32)
    up = jnp.dot(x[...], up_ref[...], preferred_element_type=F32)
    inner = (gate / (1.0 + jnp.exp(-gate)) * up).astype(BF16)
    acc[...] += jnp.dot(inner, down_ref[...], preferred_element_type=F32)

    @pl.when(step == pl.num_programs(0) - 1)
    def _():
        omain_ref[...] = acc[:cut].astype(BF16).reshape(omain_ref.shape)
        oextra_ref[...] = acc[cut:].astype(BF16).astype(F32).reshape(oextra_ref.shape)


def experts(main, extra, gate_proj, up_proj, down_proj):
    model, hidden = gate_proj.shape
    tile = 640
    zero3 = lambda i: (0, 0, 0)
    return pl.pallas_call(
        expert_kernel,
        grid=(hidden // tile,),
        out_shape=[
            jax.ShapeDtypeStruct(main.shape, BF16),
            jax.ShapeDtypeStruct(extra.shape, F32),
        ],
        in_specs=[
            pl.BlockSpec(main.shape, zero3),
            pl.BlockSpec(extra.shape, zero3),
            pl.BlockSpec((model, tile), lambda i: (0, i)),
            pl.BlockSpec((model, tile), lambda i: (0, i)),
            pl.BlockSpec((tile, model), lambda i: (i, 0)),
        ],
        out_specs=[pl.BlockSpec(main.shape, zero3), pl.BlockSpec(extra.shape, zero3)],
        scratch_shapes=[pltpu.VMEM((SLOTS, model), BF16), pltpu.VMEM((SLOTS, model), F32)],
        compiler_params=pltpu.CompilerParams(vmem_limit_bytes=56 << 20),
    )(main, extra, gate_proj, up_proj, down_proj)


def back_kernel(
    main_ref, extra_ref, res_ref, gate_ref, place_ref, out_ref,
    got_main, got_extra, terms, main_send, main_recv, extra_send, extra_recv,
):
    me = lax.axis_index("ea")
    greet(me)

    def main_copy(src, dev):
        return remote(main_ref.at[dev], got_main.at[src], main_send.at[dev], main_recv.at[src], dev)

    def extra_copy(src, dev):
        return remote(
            extra_ref.at[dev], got_extra.at[src], extra_send.at[dev], extra_recv.at[src], dev
        )

    def start(dev):
        main_copy(me, dev).start()
        extra_copy(me, dev).start()

    others(me, start)
    got_main[me] = main_ref[me]
    got_extra[me] = extra_ref[me]

    def finish(dev):
        main_copy(dev, dev).wait_recv()
        extra_copy(dev, dev).wait_recv()
        main_copy(me, dev).wait_send()
        extra_copy(me, dev).wait_send()

    others(me, finish)
    cut = EXPERTS * MAIN
    model = terms.shape[1]
    terms[:cut] = got_main[...].reshape(cut, model)
    terms[cut:] = got_extra[...].reshape(EXPERTS, model).astype(BF16)
    gate0 = gate_ref[:, 0:1]
    pick0 = jnp.dot(place_ref[0], terms[...], preferred_element_type=F32)
    pick1 = jnp.dot(place_ref[1], terms[...], preferred_element_type=F32)
    mixed = res_ref[...] + gate0 * pick0 + (1.0 - gate0) * pick1
    out_ref[...] = mixed.astype(BF16)


def back(main, extra, residual, gate, place):
    dma = pltpu.SemaphoreType.DMA
    return pl.pallas_call(
        back_kernel,
        out_shape=jax.ShapeDtypeStruct(residual.shape, BF16),
        in_specs=vmem(5),
        out_specs=vmem(1)[0],
        scratch_shapes=[
            pltpu.VMEM(main.shape, BF16),
            pltpu.VMEM(extra.shape, F32),
            pltpu.VMEM((SLOTS, residual.shape[1]), BF16),
            dma((NDEV,)), dma((NDEV,)), dma((NDEV,)), dma((NDEV,)),
        ],
        compiler_params=pltpu.CompilerParams(
            collective_id=1, has_side_effects=True, vmem_limit_bytes=40 << 20
        ),
    )(main, extra, residual, gate, place)


def body(
    hidden_in, queries, cache_keys, cache_values, new_keys, new_values, cache_len,
    out_proj, norm_gain, router, expert_ids, gate_proj, up_proj, down_proj,
):
    piece, seqs, model = hidden_in.shape
    attended = attend(
        cache_len, queries[0], cache_keys[0], cache_values[0], new_keys[0], new_values[0]
    )
    hidden = hidden_in.transpose(1, 0, 2).reshape(piece * seqs, model)
    ids = expert_ids.transpose(1, 0, 2).reshape(piece * seqs, TOPK)
    residual, gate, place, main, extra = front(
        attended, out_proj, hidden, norm_gain.reshape(1, model), router, ids
    )
    main, extra = experts(main, extra, gate_proj, up_proj, down_proj)
    out = back(main, extra, residual, gate, place)
    return out.reshape(seqs, piece, model).transpose(1, 0, 2)


def solution(mesh):
    placed = (
        P("ea", "rep", None),
        P(("rep", "ea"), None, None),
        P(("rep", "ea"), None, None),
        P(("rep", "ea"), None, None),
        P(("rep", "ea"), None, None),
        P(("rep", "ea"), None, None),
        P("rep"),
        P(None, "ea"),
        P(),
        P(),
        P("ea", "rep", None),
        P(None, "ea"),
        P(None, "ea"),
        P("ea", None),
    )
    plan = body if mesh.shape["ea"] == NDEV else wide_body
    return jax.shard_map(
        plan, mesh=mesh, in_specs=placed, out_specs=P("ea", "rep", None), check_vma=False
    )
```

```python
import functools
import math

import jax
import jax.numpy as jnp
from jax import lax
from jax.experimental import pallas as pl
from jax.experimental.pallas import tpu as pltpu
from jax.sharding import PartitionSpec as P

HQ = 32
KVH = 8
HD = 128
EXPERTS = 16
TOPK = 2
CAP = 9


def expert_terms(received, gate_proj, up_proj, down_proj):
    src_count, slot_count, model_width = received.shape
    flat_rows = received.reshape(src_count * slot_count, model_width)
    gate_val = jnp.dot(flat_rows, gate_proj, preferred_element_type=jnp.float32)
    up_val = jnp.dot(flat_rows, up_proj, preferred_element_type=jnp.float32)
    inner_act = (jax.nn.silu(gate_val) * up_val).astype(jnp.bfloat16)
    shard_term = jnp.dot(inner_act, down_proj, preferred_element_type=jnp.float32).astype(
        jnp.bfloat16
    )
    return shard_term.reshape(src_count, slot_count, model_width)


def expert_half(received, gate_proj, up_proj, down_proj):
    shard_term = expert_terms(received, gate_proj, up_proj, down_proj)
    return lax.all_to_all(shard_term, "ea", split_axis=0, concat_axis=0, tiled=True)


def route_rows(normed, route_ids, first_gate, gate_proj, up_proj, down_proj):
    row_count, model_width = normed.shape
    dev_count = lax.axis_size("ea")
    shard_count = dev_count // EXPERTS
    flat_ids = route_ids.reshape(-1)
    pair_count = flat_ids.shape[0]
    expert_cols = jnp.arange(EXPERTS, dtype=jnp.int32)
    one_hot = (flat_ids[:, None] == expert_cols[None, :]).astype(jnp.float32)
    pair_order = jnp.arange(pair_count, dtype=jnp.int32)
    earlier = (pair_order[:, None] > pair_order[None, :]).astype(jnp.float32)
    before = jnp.dot(earlier, one_hot, precision=lax.Precision.HIGHEST)
    slot_pos = jnp.sum(before * one_hot, axis=1).astype(jnp.int32)
    target = (flat_ids * CAP + slot_pos).reshape(row_count, TOPK)
    slot_ids = jnp.arange(EXPERTS * CAP, dtype=jnp.int32)
    select = (
        (target[None, :, 0] == slot_ids[:, None]) | (target[None, :, 1] == slot_ids[:, None])
    ).astype(jnp.bfloat16)
    packed = jnp.dot(select, normed, preferred_element_type=jnp.float32).astype(jnp.bfloat16)
    packed = jnp.broadcast_to(
        packed.reshape(EXPERTS, 1, CAP, model_width), (EXPERTS, shard_count, CAP, model_width)
    )
    packed = packed.reshape(dev_count, CAP, model_width)
    first_slots = (CAP + 1) // 2
    bounds = [(0, first_slots), (first_slots, CAP)]
    pieces = []
    for lower, upper in bounds:
        part_block = packed[:, lower:upper]
        pieces.append(
            (lambda received: expert_half(received, gate_proj, up_proj, down_proj))(
                lax.all_to_all(part_block, "ea", split_axis=0, concat_axis=0, tiled=True)
            )
        )
    returned = jnp.concatenate(pieces, axis=1)
    expert_out = jnp.sum(
        returned.reshape(EXPERTS, shard_count, CAP, model_width).astype(jnp.float32), axis=1
    )
    expert_out = expert_out.reshape(EXPERTS * CAP, model_width)
    picked = jnp.take(expert_out, target, axis=0)
    return first_gate * picked[:, 0] + (1.0 - first_gate) * picked[:, 1]


def wide_body(
    hidden_in,
    queries,
    cache_keys,
    cache_values,
    new_keys,
    new_values,
    cache_len,
    out_proj,
    norm_gain,
    router,
    expert_ids,
    gate_proj,
    up_proj,
    down_proj,
):
    dev_count = lax.axis_size("ea")
    dev_index = lax.axis_index("ea")
    new_rows = queries.shape[1]
    group_q = HQ // KVH
    seq_count = dev_count // KVH
    piece_rows = new_rows // dev_count
    cache_rows = cache_keys.shape[1]
    col_width = out_proj.shape[1]
    model_width = hidden_in.shape[2]
    score_scale = 1.0 / math.sqrt(HD)
    visible = lax.dynamic_index_in_dim(cache_len, dev_index // KVH, keepdims=False)
    position = (
        jnp.arange(new_rows, dtype=jnp.int32).reshape(dev_count, piece_rows).T.reshape(new_rows)
    )
    query_rows = (
        queries[0]
        .reshape(dev_count, piece_rows, group_q, HD)
        .transpose(1, 0, 2, 3)
        .reshape(new_rows, group_q, HD)
    )
    all_keys = jnp.concatenate([cache_keys[0], new_keys[0]], axis=0)
    all_values = jnp.concatenate([cache_values[0], new_values[0]], axis=0)
    key_pos = jnp.arange(cache_rows + new_rows, dtype=jnp.int32)
    allowed = jnp.where(
        key_pos[None, :] < cache_rows,
        key_pos[None, :] < visible,
        key_pos[None, :] - cache_rows <= position[:, None],
    )
    scores = (
        jnp.einsum("qhd,kd->hqk", query_rows, all_keys, preferred_element_type=jnp.float32)
        * score_scale
    )
    scores = jnp.where(allowed[None], scores, jnp.float32(-1e30))
    top_score = jnp.max(scores, axis=2, keepdims=True)
    exp_scores = jnp.exp(scores - top_score)
    attn_probs = (exp_scores / jnp.sum(exp_scores, axis=2, keepdims=True)).astype(jnp.bfloat16)
    attended = jnp.einsum("hqk,kd->qhd", attn_probs, all_values, preferred_element_type=jnp.float32)
    attended = attended.astype(jnp.bfloat16).reshape(new_rows, group_q * HD)
    local_rows = out_proj.reshape(KVH, group_q * HD, col_width).transpose(1, 0, 2)
    outgoing = jnp.broadcast_to(local_rows[:, None], (group_q * HD, seq_count, KVH, col_width))
    outgoing = outgoing.reshape(group_q * HD, dev_count, col_width)
    group_proj = lax.all_to_all(outgoing, "ea", split_axis=1, concat_axis=1, tiled=True).reshape(
        group_q * HD, model_width
    )
    head_part = jnp.dot(attended, group_proj, preferred_element_type=jnp.float32).astype(
        jnp.bfloat16
    )
    arrived = lax.all_to_all(
        head_part.reshape(piece_rows, dev_count, model_width),
        "ea",
        split_axis=1,
        concat_axis=1,
        tiled=True,
    )
    head_sum = jnp.sum(
        arrived.reshape(piece_rows, seq_count, KVH, model_width).astype(jnp.float32), axis=2
    )
    residual = hidden_in.astype(jnp.float32) + head_sum
    flat_res = residual.reshape(piece_rows * seq_count, model_width)
    mean_sq = jnp.mean(flat_res * flat_res, axis=1, keepdims=True)
    normed = (flat_res * lax.rsqrt(mean_sq + 1e-05) * norm_gain[None, :]).astype(jnp.bfloat16)
    logits = jnp.dot(normed, router, preferred_element_type=jnp.float32)
    route_ids = expert_ids.reshape(piece_rows * seq_count, TOPK)
    chosen = jnp.take_along_axis(logits, route_ids, axis=1)
    first_gate = jax.nn.sigmoid(chosen[:, 0:1] - chosen[:, 1:2])
    expert_mix = route_rows(normed, route_ids, first_gate, gate_proj, up_proj, down_proj)
    result_rows = (flat_res + expert_mix).astype(jnp.bfloat16)
    return result_rows.reshape(piece_rows, seq_count, model_width)


NZ = 4
NDEV = 16
MAIN = 8
SLOTS = EXPERTS * CAP
F32 = jnp.float32
BF16 = jnp.bfloat16


def attend_kernel(len_ref, q_ref, ck_ref, cv_ref, nk_ref, nv_ref, o_ref, *, seq_devs):
    visible = len_ref[lax.axis_index("ea") // seq_devs]
    contract = (((1,), (1,)), ((), ()))
    q = q_ref[...]
    rows, cached, fresh = q.shape[0], ck_ref.shape[0], nk_ref.shape[0]
    scale = 1.0 / math.sqrt(HD)
    old = lax.dot_general(q, ck_ref[...], contract, preferred_element_type=F32) * scale
    new = lax.dot_general(q, nk_ref[...], contract, preferred_element_type=F32) * scale
    old_pos = lax.broadcasted_iota(jnp.int32, (rows, cached), 1)
    row_pos = lax.broadcasted_iota(jnp.int32, (rows, fresh), 0)
    new_pos = lax.broadcasted_iota(jnp.int32, (rows, fresh), 1)
    old = jnp.where(old_pos < visible, old, -1e30)
    new = jnp.where(new_pos <= row_pos, new, -1e30)
    top = jnp.maximum(
        jnp.max(old, axis=1, keepdims=True), jnp.max(new, axis=1, keepdims=True)
    )
    old = jnp.exp(old - top)
    new = jnp.exp(new - top)
    total = jnp.sum(old, axis=1, keepdims=True) + jnp.sum(new, axis=1, keepdims=True)
    mixed = jnp.dot(old.astype(BF16), cv_ref[...], preferred_element_type=F32)
    mixed += jnp.dot(new.astype(BF16), nv_ref[...], preferred_element_type=F32)
    o_ref[...] = (mixed / total).astype(BF16)


def attend(cache_len, q, ck, cv, nk, nv):
    rows, width = q.shape
    return pl.pallas_call(
        functools.partial(attend_kernel, seq_devs=KVH),
        grid=(width // HD,),
        out_shape=jax.ShapeDtypeStruct((rows, width), BF16),
        in_specs=[
            pl.BlockSpec(memory_space=pltpu.SMEM),
            pl.BlockSpec((rows, HD), lambda h: (0, h)),
            pl.BlockSpec(ck.shape, lambda h: (0, 0)),
            pl.BlockSpec(cv.shape, lambda h: (0, 0)),
            pl.BlockSpec(nk.shape, lambda h: (0, 0)),
            pl.BlockSpec(nv.shape, lambda h: (0, 0)),
        ],
        out_specs=pl.BlockSpec((rows, HD), lambda h: (0, h)),
        compiler_params=pltpu.CompilerParams(vmem_limit_bytes=40 << 20),
    )(cache_len, q, ck, cv, nk, nv)


def remote(src, dst, send, recv, dev):
    return pltpu.make_async_remote_copy(
        src_ref=src,
        dst_ref=dst,
        send_sem=send,
        recv_sem=recv,
        device_id={"ea": dev},
        device_id_type=pl.DeviceIdType.MESH,
    )


def greet(me):
    barrier = pltpu.get_barrier_semaphore()

    def hello(off, carry):
        pl.semaphore_signal(
            barrier,
            inc=1,
            device_id={"ea": lax.rem(me + off, NDEV)},
            device_id_type=pl.DeviceIdType.MESH,
        )
        return carry

    lax.fori_loop(1, NDEV, hello, 0)
    pl.semaphore_wait(barrier, NDEV - 1)


def others(me, step):
    def go(off, carry):
        step(lax.rem(me + off, NDEV))
        return carry

    lax.fori_loop(1, NDEV, go, 0)


TILE = 640
TILES = 5
GU_SLOTS = 3
DN_SLOTS = 2
BACK = 1024


def layer_kernel(
    att_ref, proj_hbm, hid_hbm, gain_ref, router_hbm, ids_ref, gate_hbm, up_hbm, down_hbm,
    out_ref,
    buf, acc, hs, arrived, normed, proj_ref, hid_ref, router_ref, res_ref, gate_ref, place_ref,
    out_go, out_got, x, gacc, uacc, inner, back_go, back_got, fold, fold_back, terms, gu, dn,
    in_sem, gu_sem, dn_sem,
    block_sem, left_sem, right_sem, y_sem, core_sem,
    hs_send, hs_recv, go_send, go_recv, back_send, back_recv,
):
    me = lax.axis_index("ea")
    half = x.shape[2]
    cut = EXPERTS * MAIN
    z, y, c = me // 4, (me // 2) % 2, me % 2

    def index(zz, yy, cc):
        return (zz * 2 + yy) * 2 + cc

    def fetch(src, dst, slot):
        return pltpu.make_async_copy(src, dst, in_sem.at[slot])

    loads = [(proj_hbm, proj_ref), (hid_hbm, hid_ref), (router_hbm, router_ref)]
    for slot, (src, dst) in enumerate(loads):
        fetch(src, dst, slot).start()

    def gate_up(u):
        h, t, slot = u // TILES, u % TILES, u % GU_SLOTS
        rows = pl.ds(pl.multiple_of(h * half, half), half)
        cols = pl.ds(pl.multiple_of(t * TILE, TILE), TILE)
        return [
            pltpu.make_async_copy(src.at[rows, cols], gu.at[slot, n], gu_sem.at[slot, n])
            for n, src in enumerate((gate_hbm, up_hbm))
        ]

    def down(n):
        cols = pl.ds(pl.multiple_of(n * BACK, BACK), BACK)
        slot = n % DN_SLOTS
        return pltpu.make_async_copy(down_hbm.at[:, cols], dn.at[slot], dn_sem.at[slot])

    for u in range(GU_SLOTS):
        for copy in gate_up(u):
            copy.start()
    for n in range(DN_SLOTS):
        down(n).start()
    buf[me] = att_ref[...]
    acc[...] = jnp.zeros_like(acc)
    greet(me)

    def block_copy(blk, sem, dev):
        return remote(buf.at[blk], buf.at[blk], sem, block_sem.at[blk], dev)

    def to_left(zz):
        return block_copy(index(zz, y, c), left_sem.at[zz], index(z - 1, y, c))

    def to_right(zz):
        return block_copy(index(zz, y, c), right_sem.at[zz], index(z + 1, y, c))

    def to_y(zz):
        return block_copy(index(zz, y, c), y_sem.at[zz], index(z, 1 - y, c))

    def to_core(zz, yy):
        return block_copy(index(zz, yy, c), core_sem.at[zz * 2 + yy], index(z, y, 1 - c))

    def landed(blk):
        remote(buf.at[blk], buf.at[blk], left_sem.at[0], block_sem.at[blk], index(z, y, 1 - c)).wait_recv()

    def line(zz, go_left, go_right):
        if go_left:
            @pl.when(z > 0)
            def _():
                to_left(zz).start()
        if go_right:
            @pl.when(z < NZ - 1)
            def _():
                to_right(zz).start()
        to_y(zz).start()
        to_core(zz, y).start()

    def pair(d, step):
        @pl.when(z + d < NZ)
        def _():
            step(z + d, True)

        @pl.when(z - d >= 0)
        def _():
            step(z - d, False)

    def arrive_line(d):
        def step(zz, from_right):
            landed(index(zz, y, c))
            line(zz, from_right, not from_right)

        pair(d, step)

    def across(zz):
        landed(index(zz, 1 - y, c))
        to_core(zz, 1 - y).start()

    def arrive_y(d):
        if d == 0:
            across(z)
        else:
            pair(d, lambda zz, _: across(zz))

    def multiply(d):
        def go(n, carry):
            side, yy, cc = n % 2, (n // 2) % 2, n // 4
            zz = z + d * (1 - 2 * side)
            ok = (zz >= 0) & (zz < NZ)
            if d == 0:
                ok = ok & (side == 0)

            @pl.when(ok)
            def _():
                blk = index(zz, (y + yy) % 2, (c + cc) % 2)

                @pl.when(cc == 1)
                def _():
                    landed(blk)

                group = blk % KVH
                width = buf.shape[2]
                rows = pl.ds(pl.multiple_of(group * width, width), width)
                acc[blk // KVH] += jnp.dot(
                    buf[blk], proj_ref[rows, :], preferred_element_type=F32
                )

            return carry

        lax.fori_loop(0, 8, go, 0)

    line(z, True, True)

    ids = ids_ref[...]
    lanes = lax.broadcasted_iota(jnp.int32, (ids.shape[0], EXPERTS), 1)
    count = ids.shape[0]
    first = (ids[:, 0:1] == lanes).astype(F32)
    second = (ids[:, 1:2] == lanes).astype(F32)
    tri = (
        lax.broadcasted_iota(jnp.int32, (count, count), 1)
        < lax.broadcasted_iota(jnp.int32, (count, count), 0)
    ).astype(F32)
    before0 = jnp.dot(tri, first, preferred_element_type=F32)
    before1 = jnp.dot(tri, second, preferred_element_type=F32) + jnp.sum(
        first, axis=0, keepdims=True
    )
    slot_lanes = lax.broadcasted_iota(jnp.int32, (count, SLOTS), 1).astype(F32)

    def placing(before, one_hot, col):
        slot = jnp.sum(before * one_hot, axis=1, keepdims=True)
        expert = ids[:, col : col + 1].astype(F32)
        where = jnp.where(slot < MAIN - 0.5, expert * MAIN + slot, EXPERTS * MAIN + expert)
        return (slot_lanes == where).astype(F32)

    place0 = placing(before0, first, 0)
    place1 = placing(before1, second, 1)
    place_ref[0] = place0.astype(BF16)
    place_ref[1] = place1.astype(BF16)
    fetch(proj_hbm, proj_ref, 0).wait()

    for d in range(1, NZ):
        arrive_line(d)
        arrive_y(d - 1)
        multiply(d - 1)
    arrive_y(NZ - 1)
    multiply(NZ - 1)

    hs[...] = acc[...].astype(BF16)
    piece = arrived.shape[1]
    width = hs.shape[2]
    col_me = pl.ds(pl.multiple_of(me * width, width), width)
    row_me = pl.ds(pl.multiple_of(me * piece, piece), piece)

    def hs_copy(dev):
        rows = pl.ds(pl.multiple_of(dev * piece, piece), piece)
        return remote(
            hs.at[:, rows, :], arrived.at[:, :, col_me], hs_send.at[dev], hs_recv.at[me], dev
        )

    def hs_landed(dev):
        cols = pl.ds(pl.multiple_of(dev * width, width), width)
        remote(
            hs.at[:, row_me, :], arrived.at[:, :, cols], hs_send.at[dev], hs_recv.at[dev], dev
        ).wait_recv()

    others(me, lambda dev: hs_copy(dev).start())
    arrived[:, :, col_me] = hs[:, row_me, :]
    others(me, hs_landed)

    fetch(hid_hbm, hid_ref, 1).wait()
    fetch(router_hbm, router_ref, 2).wait()
    total = arrived[...].astype(F32).reshape(res_ref.shape)
    residual = hid_ref[...].astype(F32) + total
    res_ref[...] = residual
    mean_sq = jnp.mean(residual * residual, axis=1, keepdims=True)
    normed[...] = (residual * lax.rsqrt(mean_sq + 1e-05) * gain_ref[...]).astype(BF16)
    select = (place0 + place1).T.astype(BF16)

    def pack(store, fold_ref, values, wide):
        part = wide // MAIN
        for q in range(MAIN):
            fold_ref[:, q, :] = values[cut:, q * part : (q + 1) * part]
        store[:, :, :wide] = values[:cut].astype(BF16).reshape(NDEV, MAIN, wide)
        store[:, :, wide:] = fold_ref[...].astype(BF16)

    def unpack(store, fold_ref, place, wide):
        part = wide // MAIN
        place[:cut] = store[:, :, :wide].reshape(cut, wide)
        fold_ref[...] = store[:, :, wide:].astype(F32)
        for q in range(MAIN):
            place[cut:, q * part : (q + 1) * part] = fold_ref[:, q, :].astype(BF16)

    def go_copy(h, src, dev):
        return remote(
            out_go.at[h, dev], out_got.at[h, src], go_send.at[h, dev], go_recv.at[h, src], dev
        )

    def back_copy(n, src, dev):
        return remote(
            back_go.at[n, dev], back_got.at[n, src], back_send.at[n, dev], back_recv.at[n, src], dev
        )

    for h in range(2):
        packed = jnp.dot(
            select, normed[:, h * half : (h + 1) * half], preferred_element_type=F32
        )
        pack(out_go.at[h], fold, packed, half)
        others(me, lambda dev: go_copy(h, me, dev).start())
        out_got[h, me] = out_go[h, me]

    logits = lax.dot_general(
        normed[...], router_ref[...], (((1,), (1,)), ((), ())), preferred_element_type=F32
    )
    gap = jnp.sum(logits * first, axis=1, keepdims=True) - jnp.sum(
        logits * second, axis=1, keepdims=True
    )
    gate_ref[...] = jnp.broadcast_to(jax.nn.sigmoid(gap), gate_ref.shape)

    for h in range(2):
        others(me, lambda dev: go_copy(h, dev, dev).wait_recv())
        unpack(out_got.at[h], fold, x.at[h], half)

        def tile_step(t, carry):
            u = h * TILES + t
            slot = u % GU_SLOTS
            for copy in gate_up(u):
                copy.wait()
            gate = jnp.dot(x[h], gu[slot, 0], preferred_element_type=F32)
            up = jnp.dot(x[h], gu[slot, 1], preferred_element_type=F32)
            if h == 0:
                gacc[t] = gate
                uacc[t] = up
            else:
                gate = gacc[t] + gate
                up = uacc[t] + up
                cols = pl.ds(pl.multiple_of(t * TILE, TILE), TILE)
                inner[:, cols] = (gate / (1.0 + jnp.exp(-gate)) * up).astype(BF16)

            @pl.when(u + GU_SLOTS < 2 * TILES)
            def _():
                for copy in gate_up(u + GU_SLOTS):
                    copy.start()

            return carry

        lax.fori_loop(0, TILES, tile_step, 0)

    chunks = back_go.shape[0]

    def down_step(n, carry):
        down(n).wait()
        pack(
            back_go.at[n],
            fold_back,
            jnp.dot(inner[...], dn[n % DN_SLOTS], preferred_element_type=F32),
            BACK,
        )
        others(me, lambda dev: back_copy(n, me, dev).start())
        back_got[n, me] = back_go[n, me]

        @pl.when(n + DN_SLOTS < chunks)
        def _():
            down(n + DN_SLOTS).start()

        return carry

    lax.fori_loop(0, chunks, down_step, 0)

    gate0 = gate_ref[:, 0:1]

    def combine(n, carry):
        others(me, lambda dev: back_copy(n, dev, dev).wait_recv())
        unpack(back_got.at[n], fold_back, terms, BACK)
        cols = pl.ds(pl.multiple_of(n * BACK, BACK), BACK)
        pick0 = jnp.dot(place_ref[0], terms[...], preferred_element_type=F32)
        pick1 = jnp.dot(place_ref[1], terms[...], preferred_element_type=F32)
        mixed = res_ref[:, cols] + gate0 * pick0 + (1.0 - gate0) * pick1
        out_ref[:, cols] = mixed.astype(BF16)
        return carry

    lax.fori_loop(0, chunks, combine, 0)

    def finish(dev):
        hs_copy(dev).wait_send()
        for h in range(2):
            go_copy(h, me, dev).wait_send()

        def sent(n, carry):
            back_copy(n, me, dev).wait_send()
            return carry

        lax.fori_loop(0, chunks, sent, 0)

    others(me, finish)
    for zz in range(NZ):
        @pl.when((z > 0) & (zz >= z))
        def _():
            to_left(zz).wait_send()

        @pl.when((z < NZ - 1) & (zz <= z))
        def _():
            to_right(zz).wait_send()

        to_y(zz).wait_send()
        to_core(zz, 0).wait_send()
        to_core(zz, 1).wait_send()


def layer(attended, out_proj, hidden, gain, router, ids, gate_proj, up_proj, down_proj):
    rows, width = attended.shape
    seqs = NDEV // KVH
    cols = out_proj.shape[1]
    mine, model = hidden.shape
    ffw = gate_proj.shape[1]
    half, chunks = model // 2, model // BACK
    dma = pltpu.SemaphoreType.DMA
    inside = pl.BlockSpec(memory_space=pltpu.VMEM)
    outside = pl.BlockSpec(memory_space=pl.ANY)
    go = (2, NDEV, MAIN, half + half // MAIN)
    back = (chunks, NDEV, MAIN, BACK + BACK // MAIN)
    return pl.pallas_call(
        layer_kernel,
        out_shape=jax.ShapeDtypeStruct((mine, model), BF16),
        in_specs=[inside, outside, outside, inside, outside, inside] + [outside] * 3,
        out_specs=inside,
        scratch_shapes=[
            pltpu.VMEM((NDEV, rows, width), BF16),
            pltpu.VMEM((seqs, rows, cols), F32),
            pltpu.VMEM((seqs, rows, cols), BF16),
            pltpu.VMEM((seqs, rows // NDEV, model), BF16),
            pltpu.VMEM((mine, model), BF16),
            pltpu.VMEM(out_proj.shape, BF16),
            pltpu.VMEM(hidden.shape, BF16),
            pltpu.VMEM(router.shape, BF16),
            pltpu.VMEM((mine, model), F32),
            pltpu.VMEM((mine, 128), F32),
            pltpu.VMEM((2, mine, SLOTS), BF16),
            pltpu.VMEM(go, BF16),
            pltpu.VMEM(go, BF16),
            pltpu.VMEM((2, SLOTS, half), BF16),
            pltpu.VMEM((TILES, SLOTS, TILE), F32),
            pltpu.VMEM((TILES, SLOTS, TILE), F32),
            pltpu.VMEM((SLOTS, ffw), BF16),
            pltpu.VMEM(back, BF16),
            pltpu.VMEM(back, BF16),
            pltpu.VMEM((NDEV, MAIN, half // MAIN), F32),
            pltpu.VMEM((NDEV, MAIN, BACK // MAIN), F32),
            pltpu.VMEM((SLOTS, BACK), BF16),
            pltpu.VMEM((GU_SLOTS, 2, half, TILE), BF16),
            pltpu.VMEM((DN_SLOTS, ffw, BACK), BF16),
            dma((3,)), dma((GU_SLOTS, 2)), dma((DN_SLOTS,)),
            dma((NDEV,)), dma((NZ,)), dma((NZ,)), dma((NZ,)), dma((2 * NZ,)),
            dma((NDEV,)), dma((NDEV,)), dma((2, NDEV)), dma((2, NDEV)),
            dma((chunks, NDEV)), dma((chunks, NDEV)),
        ],
        compiler_params=pltpu.CompilerParams(
            collective_id=0, has_side_effects=True, vmem_limit_bytes=62 << 20
        ),
    )(attended, out_proj, hidden, gain, router, ids, gate_proj, up_proj, down_proj)


def body(
    hidden_in, queries, cache_keys, cache_values, new_keys, new_values, cache_len,
    out_proj, norm_gain, router, expert_ids, gate_proj, up_proj, down_proj,
):
    piece, seqs, model = hidden_in.shape
    attended = attend(
        cache_len, queries[0], cache_keys[0], cache_values[0], new_keys[0], new_values[0]
    )
    hidden = hidden_in.transpose(1, 0, 2).reshape(piece * seqs, model)
    ids = expert_ids.transpose(1, 0, 2).reshape(piece * seqs, TOPK)
    out = layer(
        attended, out_proj, hidden, norm_gain.reshape(1, model), router.T, ids,
        gate_proj, up_proj, down_proj,
    )
    return out.reshape(seqs, piece, model).transpose(1, 0, 2)


def solution(mesh):
    placed = (
        P("ea", "rep", None),
        P(("rep", "ea"), None, None),
        P(("rep", "ea"), None, None),
        P(("rep", "ea"), None, None),
        P(("rep", "ea"), None, None),
        P(("rep", "ea"), None, None),
        P("rep"),
        P(None, "ea"),
        P(),
        P(),
        P("ea", "rep", None),
        P(None, "ea"),
        P(None, "ea"),
        P("ea", None),
    )
    plan = body if mesh.shape["ea"] == NDEV else wide_body
    return jax.shard_map(
        plan, mesh=mesh, in_specs=placed, out_specs=P("ea", "rep", None), check_vma=False
    )
```

```python
import functools
import math

import jax
import jax.numpy as jnp
from jax import lax
from jax.experimental import pallas as pl
from jax.experimental.pallas import tpu as pltpu
from jax.sharding import PartitionSpec as P

HQ = 32
KVH = 8
HD = 128
EXPERTS = 16
TOPK = 2
CAP = 9


def expert_terms(received, gate_proj, up_proj, down_proj):
    src_count, slot_count, model_width = received.shape
    flat_rows = received.reshape(src_count * slot_count, model_width)
    gate_val = jnp.dot(flat_rows, gate_proj, preferred_element_type=jnp.float32)
    up_val = jnp.dot(flat_rows, up_proj, preferred_element_type=jnp.float32)
    inner_act = (jax.nn.silu(gate_val) * up_val).astype(jnp.bfloat16)
    shard_term = jnp.dot(inner_act, down_proj, preferred_element_type=jnp.float32).astype(
        jnp.bfloat16
    )
    return shard_term.reshape(src_count, slot_count, model_width)


def expert_half(received, gate_proj, up_proj, down_proj):
    shard_term = expert_terms(received, gate_proj, up_proj, down_proj)
    return lax.all_to_all(shard_term, "ea", split_axis=0, concat_axis=0, tiled=True)


def route_rows(normed, route_ids, first_gate, gate_proj, up_proj, down_proj):
    row_count, model_width = normed.shape
    dev_count = lax.axis_size("ea")
    shard_count = dev_count // EXPERTS
    flat_ids = route_ids.reshape(-1)
    pair_count = flat_ids.shape[0]
    expert_cols = jnp.arange(EXPERTS, dtype=jnp.int32)
    one_hot = (flat_ids[:, None] == expert_cols[None, :]).astype(jnp.float32)
    pair_order = jnp.arange(pair_count, dtype=jnp.int32)
    earlier = (pair_order[:, None] > pair_order[None, :]).astype(jnp.float32)
    before = jnp.dot(earlier, one_hot, precision=lax.Precision.HIGHEST)
    slot_pos = jnp.sum(before * one_hot, axis=1).astype(jnp.int32)
    target = (flat_ids * CAP + slot_pos).reshape(row_count, TOPK)
    slot_ids = jnp.arange(EXPERTS * CAP, dtype=jnp.int32)
    select = (
        (target[None, :, 0] == slot_ids[:, None]) | (target[None, :, 1] == slot_ids[:, None])
    ).astype(jnp.bfloat16)
    packed = jnp.dot(select, normed, preferred_element_type=jnp.float32).astype(jnp.bfloat16)
    packed = jnp.broadcast_to(
        packed.reshape(EXPERTS, 1, CAP, model_width), (EXPERTS, shard_count, CAP, model_width)
    )
    packed = packed.reshape(dev_count, CAP, model_width)
    first_slots = (CAP + 1) // 2
    bounds = [(0, first_slots), (first_slots, CAP)]
    pieces = []
    for lower, upper in bounds:
        part_block = packed[:, lower:upper]
        pieces.append(
            (lambda received: expert_half(received, gate_proj, up_proj, down_proj))(
                lax.all_to_all(part_block, "ea", split_axis=0, concat_axis=0, tiled=True)
            )
        )
    returned = jnp.concatenate(pieces, axis=1)
    expert_out = jnp.sum(
        returned.reshape(EXPERTS, shard_count, CAP, model_width).astype(jnp.float32), axis=1
    )
    expert_out = expert_out.reshape(EXPERTS * CAP, model_width)
    picked = jnp.take(expert_out, target, axis=0)
    return first_gate * picked[:, 0] + (1.0 - first_gate) * picked[:, 1]


def wide_body(
    hidden_in,
    queries,
    cache_keys,
    cache_values,
    new_keys,
    new_values,
    cache_len,
    out_proj,
    norm_gain,
    router,
    expert_ids,
    gate_proj,
    up_proj,
    down_proj,
):
    dev_count = lax.axis_size("ea")
    dev_index = lax.axis_index("ea")
    new_rows = queries.shape[1]
    group_q = HQ // KVH
    seq_count = dev_count // KVH
    piece_rows = new_rows // dev_count
    cache_rows = cache_keys.shape[1]
    col_width = out_proj.shape[1]
    model_width = hidden_in.shape[2]
    score_scale = 1.0 / math.sqrt(HD)
    visible = lax.dynamic_index_in_dim(cache_len, dev_index // KVH, keepdims=False)
    position = (
        jnp.arange(new_rows, dtype=jnp.int32).reshape(dev_count, piece_rows).T.reshape(new_rows)
    )
    query_rows = (
        queries[0]
        .reshape(dev_count, piece_rows, group_q, HD)
        .transpose(1, 0, 2, 3)
        .reshape(new_rows, group_q, HD)
    )
    all_keys = jnp.concatenate([cache_keys[0], new_keys[0]], axis=0)
    all_values = jnp.concatenate([cache_values[0], new_values[0]], axis=0)
    key_pos = jnp.arange(cache_rows + new_rows, dtype=jnp.int32)
    allowed = jnp.where(
        key_pos[None, :] < cache_rows,
        key_pos[None, :] < visible,
        key_pos[None, :] - cache_rows <= position[:, None],
    )
    scores = (
        jnp.einsum("qhd,kd->hqk", query_rows, all_keys, preferred_element_type=jnp.float32)
        * score_scale
    )
    scores = jnp.where(allowed[None], scores, jnp.float32(-1e30))
    top_score = jnp.max(scores, axis=2, keepdims=True)
    exp_scores = jnp.exp(scores - top_score)
    attn_probs = (exp_scores / jnp.sum(exp_scores, axis=2, keepdims=True)).astype(jnp.bfloat16)
    attended = jnp.einsum("hqk,kd->qhd", attn_probs, all_values, preferred_element_type=jnp.float32)
    attended = attended.astype(jnp.bfloat16).reshape(new_rows, group_q * HD)
    local_rows = out_proj.reshape(KVH, group_q * HD, col_width).transpose(1, 0, 2)
    outgoing = jnp.broadcast_to(local_rows[:, None], (group_q * HD, seq_count, KVH, col_width))
    outgoing = outgoing.reshape(group_q * HD, dev_count, col_width)
    group_proj = lax.all_to_all(outgoing, "ea", split_axis=1, concat_axis=1, tiled=True).reshape(
        group_q * HD, model_width
    )
    head_part = jnp.dot(attended, group_proj, preferred_element_type=jnp.float32).astype(
        jnp.bfloat16
    )
    arrived = lax.all_to_all(
        head_part.reshape(piece_rows, dev_count, model_width),
        "ea",
        split_axis=1,
        concat_axis=1,
        tiled=True,
    )
    head_sum = jnp.sum(
        arrived.reshape(piece_rows, seq_count, KVH, model_width).astype(jnp.float32), axis=2
    )
    residual = hidden_in.astype(jnp.float32) + head_sum
    flat_res = residual.reshape(piece_rows * seq_count, model_width)
    mean_sq = jnp.mean(flat_res * flat_res, axis=1, keepdims=True)
    normed = (flat_res * lax.rsqrt(mean_sq + 1e-05) * norm_gain[None, :]).astype(jnp.bfloat16)
    logits = jnp.dot(normed, router, preferred_element_type=jnp.float32)
    route_ids = expert_ids.reshape(piece_rows * seq_count, TOPK)
    chosen = jnp.take_along_axis(logits, route_ids, axis=1)
    first_gate = jax.nn.sigmoid(chosen[:, 0:1] - chosen[:, 1:2])
    expert_mix = route_rows(normed, route_ids, first_gate, gate_proj, up_proj, down_proj)
    result_rows = (flat_res + expert_mix).astype(jnp.bfloat16)
    return result_rows.reshape(piece_rows, seq_count, model_width)


NZ = 4
NDEV = 16
MAIN = 8
SLOTS = EXPERTS * CAP
F32 = jnp.float32
BF16 = jnp.bfloat16


def attend(q, ck, cv, nk, nv, visible, first_row):
    contract = (((1,), (1,)), ((), ()))
    rows, cached, fresh = q.shape[0], ck.shape[0], nk.shape[0]
    scale = 1.0 / math.sqrt(HD)
    old = lax.dot_general(q, ck, contract, preferred_element_type=F32) * scale
    new = lax.dot_general(q, nk, contract, preferred_element_type=F32) * scale
    old_pos = lax.broadcasted_iota(jnp.int32, (rows, cached), 1)
    row_pos = lax.broadcasted_iota(jnp.int32, (rows, fresh), 0) + first_row
    new_pos = lax.broadcasted_iota(jnp.int32, (rows, fresh), 1)
    old = jnp.where(old_pos < visible, old, -1e30)
    new = jnp.where(new_pos <= row_pos, new, -1e30)
    top = jnp.maximum(
        jnp.max(old, axis=1, keepdims=True), jnp.max(new, axis=1, keepdims=True)
    )
    old = jnp.exp(old - top)
    new = jnp.exp(new - top)
    total = jnp.sum(old, axis=1, keepdims=True) + jnp.sum(new, axis=1, keepdims=True)
    mixed = jnp.dot(old.astype(BF16), cv, preferred_element_type=F32)
    mixed += jnp.dot(new.astype(BF16), nv, preferred_element_type=F32)
    return (mixed / total).astype(BF16)


def remote(src, dst, send, recv, dev):
    return pltpu.make_async_remote_copy(
        src_ref=src,
        dst_ref=dst,
        send_sem=send,
        recv_sem=recv,
        device_id={"ea": dev},
        device_id_type=pl.DeviceIdType.MESH,
    )


def greet(me):
    barrier = pltpu.get_barrier_semaphore()

    def hello(off, carry):
        pl.semaphore_signal(
            barrier,
            inc=1,
            device_id={"ea": lax.rem(me + off, NDEV)},
            device_id_type=pl.DeviceIdType.MESH,
        )
        return carry

    lax.fori_loop(1, NDEV, hello, 0)
    pl.semaphore_wait(barrier, NDEV - 1)


def others(me, step):
    def go(off, carry):
        step(lax.rem(me + off, NDEV))
        return carry

    lax.fori_loop(1, NDEV, go, 0)


TILE = 640
TILES = 5
GU_SLOTS = 3
DN_SLOTS = 2
PIECES = 2
BACK = 1024


def layer_kernel(
    len_ref, q_hbm, ck_hbm, cv_hbm, nk_hbm, nv_hbm, proj_hbm, hid_hbm, gain_ref, router_hbm, ids_ref, gate_hbm, up_hbm, down_hbm,
    out_ref,
    q_ref, ck_ref, cv_ref, nk_ref, nv_ref,
    buf, acc, hs, arrived, normed, proj_ref, hid_ref, router_ref, res_ref, gate_ref, place_ref,
    out_go, out_got, x, gacc, uacc, inner, back_go, back_got, fold, fold_back, terms, gu, dn,
    in_sem, gu_sem, dn_sem,
    block_sem, left_sem, right_sem, y_sem, core_sem,
    hs_send, hs_recv, go_send, go_recv, back_send, back_recv,
):
    me = lax.axis_index("ea")
    half = x.shape[2]
    cut = EXPERTS * MAIN
    z, y, c = me // 4, (me // 2) % 2, me % 2

    def index(zz, yy, cc):
        return (zz * 2 + yy) * 2 + cc

    def fetch(src, dst, slot):
        return pltpu.make_async_copy(src, dst, in_sem.at[slot])

    loads = [
        (proj_hbm, proj_ref), (hid_hbm, hid_ref), (router_hbm, router_ref),
        (q_hbm, q_ref), (ck_hbm, ck_ref), (nk_hbm, nk_ref), (cv_hbm, cv_ref), (nv_hbm, nv_ref),
    ]
    for slot in (3, 4, 5, 6, 7, 0, 1, 2):
        fetch(*loads[slot], slot).start()

    def gate_up(u):
        h, t, slot = u // TILES, u % TILES, u % GU_SLOTS
        rows = pl.ds(pl.multiple_of(h * half, half), half)
        cols = pl.ds(pl.multiple_of(t * TILE, TILE), TILE)
        return [
            pltpu.make_async_copy(src.at[rows, cols], gu.at[slot, n], gu_sem.at[slot, n])
            for n, src in enumerate((gate_hbm, up_hbm))
        ]

    def down(n):
        cols = pl.ds(pl.multiple_of(n * BACK, BACK), BACK)
        slot = n % DN_SLOTS
        return pltpu.make_async_copy(down_hbm.at[:, cols], dn.at[slot], dn_sem.at[slot])

    for u in range(GU_SLOTS):
        for copy in gate_up(u):
            copy.start()
    for n in range(DN_SLOTS):
        down(n).start()
    acc[...] = jnp.zeros_like(acc)
    greet(me)

    def block_copy(p, blk, sem, dev):
        return remote(buf.at[p, blk], buf.at[p, blk], sem, block_sem.at[p, blk], dev)

    def to_left(p, zz):
        return block_copy(p, index(zz, y, c), left_sem.at[p, zz], index(z - 1, y, c))

    def to_right(p, zz):
        return block_copy(p, index(zz, y, c), right_sem.at[p, zz], index(z + 1, y, c))

    def to_y(p, zz):
        return block_copy(p, index(zz, y, c), y_sem.at[p, zz], index(z, 1 - y, c))

    def to_core(p, zz, yy):
        return block_copy(p, index(zz, yy, c), core_sem.at[p, zz * 2 + yy], index(z, y, 1 - c))

    def landed(p, blk):
        block_copy(p, blk, left_sem.at[p, 0], index(z, y, 1 - c)).wait_recv()

    def line(p, zz, go_left, go_right):
        if go_left:
            @pl.when(z > 0)
            def _():
                to_left(p, zz).start()
        if go_right:
            @pl.when(z < NZ - 1)
            def _():
                to_right(p, zz).start()
        to_y(p, zz).start()
        to_core(p, zz, y).start()

    def pair(d, step):
        @pl.when(z + d < NZ)
        def _():
            step(z + d, True)

        @pl.when(z - d >= 0)
        def _():
            step(z - d, False)

    def arrive_line(p, d):
        def step(zz, from_right):
            landed(p, index(zz, y, c))
            line(p, zz, from_right, not from_right)

        pair(d, step)

    def across(p, zz):
        landed(p, index(zz, 1 - y, c))
        to_core(p, zz, 1 - y).start()

    def arrive_y(p, d):
        if d == 0:
            across(p, z)
        else:
            pair(d, lambda zz, _: across(p, zz))

    def multiply(d):
        def go(n, carry):
            side, yy, cc = n % 2, (n // 2) % 2, n // 4
            zz = z + d * (1 - 2 * side)
            ok = (zz >= 0) & (zz < NZ)
            if d == 0:
                ok = ok & (side == 0)

            @pl.when(ok)
            def _():
                blk = index(zz, (y + yy) % 2, (c + cc) % 2)

                @pl.when(cc == 1)
                def _():
                    for p in range(PIECES):
                        landed(p, blk)

                group = blk % KVH
                total = acc[blk // KVH]
                for p in range(PIECES):
                    start = (group * PIECES + p) * part
                    rows = pl.ds(pl.multiple_of(start, part), part)
                    total += jnp.dot(
                        buf[p, blk], proj_ref[rows, :], preferred_element_type=F32
                    )
                acc[blk // KVH] = total

            return carry

        lax.fori_loop(0, 8, go, 0)

    part = buf.shape[3]
    for slot in (3, 4, 5, 6, 7):
        fetch(*loads[slot], slot).wait()
    visible = len_ref[me // KVH]
    tall = q_ref.shape[0] // 2
    for p in range(PIECES):
        def head(n, carry):
            src = pl.ds(pl.multiple_of(p * part + n * HD, HD), HD)
            dst = pl.ds(pl.multiple_of(n * HD, HD), HD)
            for t in range(2):
                rows = slice(t * tall, (t + 1) * tall)
                keys = slice(0, (t + 1) * tall)
                buf[p, me, rows, dst] = attend(
                    q_ref[rows, src], ck_ref[...], cv_ref[...], nk_ref[keys], nv_ref[keys],
                    visible, t * tall,
                )
            return carry

        lax.fori_loop(0, part // HD, head, 0)
        line(p, z, True, True)

    ids = jnp.concatenate([ids_ref[:, 0, :], ids_ref[:, 1, :]], axis=0)
    lanes = lax.broadcasted_iota(jnp.int32, (ids.shape[0], EXPERTS), 1)
    count = ids.shape[0]
    first = (ids[:, 0:1] == lanes).astype(F32)
    second = (ids[:, 1:2] == lanes).astype(F32)
    tri = (
        lax.broadcasted_iota(jnp.int32, (count, count), 1)
        < lax.broadcasted_iota(jnp.int32, (count, count), 0)
    ).astype(F32)
    before0 = jnp.dot(tri, first, preferred_element_type=F32)
    before1 = jnp.dot(tri, second, preferred_element_type=F32) + jnp.sum(
        first, axis=0, keepdims=True
    )
    slot_lanes = lax.broadcasted_iota(jnp.int32, (count, SLOTS), 1).astype(F32)

    def placing(before, one_hot, col):
        slot = jnp.sum(before * one_hot, axis=1, keepdims=True)
        expert = ids[:, col : col + 1].astype(F32)
        where = jnp.where(slot < MAIN - 0.5, expert * MAIN + slot, EXPERTS * MAIN + expert)
        return (slot_lanes == where).astype(F32)

    place0 = placing(before0, first, 0)
    place1 = placing(before1, second, 1)
    place_ref[0] = place0.astype(BF16)
    place_ref[1] = place1.astype(BF16)
    fetch(proj_hbm, proj_ref, 0).wait()

    for d in range(1, NZ):
        for p in range(PIECES):
            arrive_line(p, d)
            arrive_y(p, d - 1)
        multiply(d - 1)
    for p in range(PIECES):
        arrive_y(p, NZ - 1)
    multiply(NZ - 1)

    hs[...] = acc[...].astype(BF16)
    piece = arrived.shape[1]
    width = hs.shape[2]
    col_me = pl.ds(pl.multiple_of(me * width, width), width)
    row_me = pl.ds(pl.multiple_of(me * piece, piece), piece)

    def hs_copy(dev):
        rows = pl.ds(pl.multiple_of(dev * piece, piece), piece)
        return remote(
            hs.at[:, rows, :], arrived.at[:, :, col_me], hs_send.at[dev], hs_recv.at[me], dev
        )

    def hs_landed(dev):
        cols = pl.ds(pl.multiple_of(dev * width, width), width)
        remote(
            hs.at[:, row_me, :], arrived.at[:, :, cols], hs_send.at[dev], hs_recv.at[dev], dev
        ).wait_recv()

    others(me, lambda dev: hs_copy(dev).start())
    arrived[:, :, col_me] = hs[:, row_me, :]
    others(me, hs_landed)

    fetch(hid_hbm, hid_ref, 1).wait()
    fetch(router_hbm, router_ref, 2).wait()
    total = arrived[...].astype(F32).reshape(res_ref.shape)
    residual = hid_ref[...].astype(F32) + total
    res_ref[...] = residual
    mean_sq = jnp.mean(residual * residual, axis=1, keepdims=True)
    normed[...] = (residual * lax.rsqrt(mean_sq + 1e-05) * gain_ref[...]).astype(BF16)
    select = (place0 + place1).T.astype(BF16)

    def pack(store, fold_ref, values, wide):
        part = wide // MAIN
        for q in range(MAIN):
            fold_ref[:, q, :] = values[cut:, q * part : (q + 1) * part]
        store[:, :, :wide] = values[:cut].astype(BF16).reshape(NDEV, MAIN, wide)
        store[:, :, wide:] = fold_ref[...].astype(BF16)

    def unpack(store, fold_ref, place, wide):
        part = wide // MAIN
        place[:cut] = store[:, :, :wide].reshape(cut, wide)
        fold_ref[...] = store[:, :, wide:].astype(F32)
        for q in range(MAIN):
            place[cut:, q * part : (q + 1) * part] = fold_ref[:, q, :].astype(BF16)

    def go_copy(h, src, dev):
        return remote(
            out_go.at[h, dev], out_got.at[h, src], go_send.at[h, dev], go_recv.at[h, src], dev
        )

    def back_copy(n, src, dev):
        return remote(
            back_go.at[n, dev], back_got.at[n, src], back_send.at[n, dev], back_recv.at[n, src], dev
        )

    for h in range(2):
        packed = jnp.dot(
            select, normed[:, h * half : (h + 1) * half], preferred_element_type=F32
        )
        pack(out_go.at[h], fold, packed, half)
        others(me, lambda dev: go_copy(h, me, dev).start())
        out_got[h, me] = out_go[h, me]

    logits = lax.dot_general(
        normed[...], router_ref[...], (((1,), (1,)), ((), ())), preferred_element_type=F32
    )
    gap = jnp.sum(logits * first, axis=1, keepdims=True) - jnp.sum(
        logits * second, axis=1, keepdims=True
    )
    gate_ref[...] = jnp.broadcast_to(jax.nn.sigmoid(gap), gate_ref.shape)

    for h in range(2):
        others(me, lambda dev: go_copy(h, dev, dev).wait_recv())
        unpack(out_got.at[h], fold, x.at[h], half)

        def tile_step(t, carry):
            u = h * TILES + t
            slot = u % GU_SLOTS
            for copy in gate_up(u):
                copy.wait()
            gate = jnp.dot(x[h], gu[slot, 0], preferred_element_type=F32)
            up = jnp.dot(x[h], gu[slot, 1], preferred_element_type=F32)
            if h == 0:
                gacc[t] = gate
                uacc[t] = up
            else:
                gate = gacc[t] + gate
                up = uacc[t] + up
                cols = pl.ds(pl.multiple_of(t * TILE, TILE), TILE)
                inner[:, cols] = (gate / (1.0 + jnp.exp(-gate)) * up).astype(BF16)

            @pl.when(u + GU_SLOTS < 2 * TILES)
            def _():
                for copy in gate_up(u + GU_SLOTS):
                    copy.start()

            return carry

        lax.fori_loop(0, TILES, tile_step, 0)

    chunks = back_go.shape[0]

    def down_step(n, carry):
        down(n).wait()
        pack(
            back_go.at[n],
            fold_back,
            jnp.dot(inner[...], dn[n % DN_SLOTS], preferred_element_type=F32),
            BACK,
        )
        others(me, lambda dev: back_copy(n, me, dev).start())
        back_got[n, me] = back_go[n, me]

        @pl.when(n + DN_SLOTS < chunks)
        def _():
            down(n + DN_SLOTS).start()

        return carry

    lax.fori_loop(0, chunks, down_step, 0)

    gate0 = gate_ref[:, 0:1]

    def combine(n, carry):
        others(me, lambda dev: back_copy(n, dev, dev).wait_recv())
        unpack(back_got.at[n], fold_back, terms, BACK)
        cols = pl.ds(pl.multiple_of(n * BACK, BACK), BACK)
        pick0 = jnp.dot(place_ref[0], terms[...], preferred_element_type=F32)
        pick1 = jnp.dot(place_ref[1], terms[...], preferred_element_type=F32)
        mixed = res_ref[:, cols] + gate0 * pick0 + (1.0 - gate0) * pick1
        out_ref[:, cols] = mixed.astype(BF16)
        return carry

    lax.fori_loop(0, chunks, combine, 0)

    def finish(dev):
        hs_copy(dev).wait_send()
        for h in range(2):
            go_copy(h, me, dev).wait_send()

        def sent(n, carry):
            back_copy(n, me, dev).wait_send()
            return carry

        lax.fori_loop(0, chunks, sent, 0)

    others(me, finish)
    for p in range(PIECES):
        for zz in range(NZ):
            @pl.when((z > 0) & (zz >= z))
            def _():
                to_left(p, zz).wait_send()

            @pl.when((z < NZ - 1) & (zz <= z))
            def _():
                to_right(p, zz).wait_send()

            to_y(p, zz).wait_send()
            to_core(p, zz, 0).wait_send()
            to_core(p, zz, 1).wait_send()


def layer(cache_len, q, ck, cv, nk, nv, out_proj, hidden, gain, router, ids, gate_proj, up_proj, down_proj):
    rows, width = q.shape
    seqs = NDEV // KVH
    cols = out_proj.shape[1]
    mine, model = hidden.shape
    ffw = gate_proj.shape[1]
    half, chunks = model // 2, model // BACK
    dma = pltpu.SemaphoreType.DMA
    inside = pl.BlockSpec(memory_space=pltpu.VMEM)
    outside = pl.BlockSpec(memory_space=pl.ANY)
    go = (2, NDEV, MAIN, half + half // MAIN)
    back = (chunks, NDEV, MAIN, BACK + BACK // MAIN)
    return pl.pallas_call(
        layer_kernel,
        out_shape=jax.ShapeDtypeStruct((mine, model), BF16),
        in_specs=[pl.BlockSpec(memory_space=pltpu.SMEM)]
        + [outside] * 7
        + [inside, outside, inside]
        + [outside] * 3,
        out_specs=inside,
        scratch_shapes=[
            pltpu.VMEM(q.shape, BF16),
            pltpu.VMEM(ck.shape, BF16),
            pltpu.VMEM(cv.shape, BF16),
            pltpu.VMEM(nk.shape, BF16),
            pltpu.VMEM(nv.shape, BF16),
            pltpu.VMEM((PIECES, NDEV, rows, width // PIECES), BF16),
            pltpu.VMEM((seqs, rows, cols), F32),
            pltpu.VMEM((seqs, rows, cols), BF16),
            pltpu.VMEM((seqs, rows // NDEV, model), BF16),
            pltpu.VMEM((mine, model), BF16),
            pltpu.VMEM(out_proj.shape, BF16),
            pltpu.VMEM(hidden.shape, BF16),
            pltpu.VMEM(router.shape, BF16),
            pltpu.VMEM((mine, model), F32),
            pltpu.VMEM((mine, 128), F32),
            pltpu.VMEM((2, mine, SLOTS), BF16),
            pltpu.VMEM(go, BF16),
            pltpu.VMEM(go, BF16),
            pltpu.VMEM((2, SLOTS, half), BF16),
            pltpu.VMEM((TILES, SLOTS, TILE), F32),
            pltpu.VMEM((TILES, SLOTS, TILE), F32),
            pltpu.VMEM((SLOTS, ffw), BF16),
            pltpu.VMEM(back, BF16),
            pltpu.VMEM(back, BF16),
            pltpu.VMEM((NDEV, MAIN, half // MAIN), F32),
            pltpu.VMEM((NDEV, MAIN, BACK // MAIN), F32),
            pltpu.VMEM((SLOTS, BACK), BF16),
            pltpu.VMEM((GU_SLOTS, 2, half, TILE), BF16),
            pltpu.VMEM((DN_SLOTS, ffw, BACK), BF16),
            dma((8,)), dma((GU_SLOTS, 2)), dma((DN_SLOTS,)), dma((PIECES, NDEV)),
            dma((PIECES, NZ)), dma((PIECES, NZ)), dma((PIECES, NZ)), dma((PIECES, 2 * NZ)),
            dma((NDEV,)), dma((NDEV,)), dma((2, NDEV)), dma((2, NDEV)),
            dma((chunks, NDEV)), dma((chunks, NDEV)),
        ],
        compiler_params=pltpu.CompilerParams(
            collective_id=0, has_side_effects=True, vmem_limit_bytes=62 << 20
        ),
    )(cache_len, q, ck, cv, nk, nv, out_proj, hidden, gain, router, ids, gate_proj, up_proj, down_proj)


def body(
    hidden_in, queries, cache_keys, cache_values, new_keys, new_values, cache_len,
    out_proj, norm_gain, router, expert_ids, gate_proj, up_proj, down_proj,
):
    piece, seqs, model = hidden_in.shape
    hidden = hidden_in.transpose(1, 0, 2).reshape(piece * seqs, model)
    out = layer(
        cache_len, queries[0], cache_keys[0], cache_values[0], new_keys[0], new_values[0],
        out_proj, hidden, norm_gain.reshape(1, model), router.T, expert_ids,
        gate_proj, up_proj, down_proj,
    )
    return out.reshape(seqs, piece, model).transpose(1, 0, 2)


def solution(mesh):
    placed = (
        P("ea", "rep", None),
        P(("rep", "ea"), None, None),
        P(("rep", "ea"), None, None),
        P(("rep", "ea"), None, None),
        P(("rep", "ea"), None, None),
        P(("rep", "ea"), None, None),
        P("rep"),
        P(None, "ea"),
        P(),
        P(),
        P("ea", "rep", None),
        P(None, "ea"),
        P(None, "ea"),
        P("ea", None),
    )
    plan = body if mesh.shape["ea"] == NDEV else wide_body
    return jax.shard_map(
        plan, mesh=mesh, in_specs=placed, out_specs=P("ea", "rep", None), check_vma=False
    )
```
